768 devices in a mesh: wide: 192 (over z, y, x_lo), narrow: 4 (over x_hi, core).
Axes of the slice: x: 4 (x_hi: 2, x_lo: 2; x = x_hi * 2 + x_lo), y: 8, z: 12, core: 2. Of those that a mesh axis runs over, the one named last changes fastest.
Arguments:
- events: bfloat16 [98304, 1024], P(('wide', 'narrow')), may hold values from -6 to 6
- buckets: int32 [98304], P('wide'), may hold values from 0 to 63
- counts: int32 [192], replicated, may hold values from 256 to 512, as said below
- prior_keys: bfloat16 [1024, 1024], P(None, 'narrow'), may hold values from -6 to 6
- prior_values: bfloat16 [1024, 1024], P(None, 'narrow'), may hold values from -6 to 6
- prior_buckets: int32 [1024], replicated, may hold values from 0 to 63
- w_input: bfloat16 [1024, 4096], replicated, may hold values from -0.1875 to 0.1875
- w_output: bfloat16 [1024, 1024], replicated, may hold values from -0.1875 to 0.1875
- time_bias: float32 [64, 16], replicated, may hold values from -4 to 4
Outputs:
- result: bfloat16 [98304, 1024], P(('wide', 'narrow'))
The draws below stay inside these ranges and needn't reach their ends.
Inputs may be any that keep to these rules, and one draw needn't show every extreme that they name: `counts`: some block is full in every draw.
All inputs are finite; a program needn't handle non-finite values.
Results may differ from the reference program's by a relative error of at most 0.0068.
Values may be sent and summed in bfloat16 or wider, within the bound.
No kernel may reach another device: no remote copies, remote signals or barrier semaphores. Data moves between devices by JAX's collectives and lax.ppermute only.
A program may use at most 64 MiB of HBM per device.

```python
import jax
import jax.numpy as jnp
from jax import lax

D = 1024
HEADS = 16
HEAD_DIM = 64
NB = 64
BLOCK = 512
BLOCKS = 192
SEQ = 98304
N_WIDE = 192


def draw_counts(key, part):
    filled = jax.random.randint(key, (BLOCKS,), BLOCK // 2, BLOCK + 1)
    chosen = jax.random.randint(jax.random.fold_in(key, 7), (), 0, BLOCKS)
    return jnp.where(jnp.arange(BLOCKS) == chosen, BLOCK, filled).astype(jnp.int32)


def set_ends(array, stream_key, least, top_value):
    index_at = [jax.random.randint(jax.random.fold_in(stream_key, axis), (), 0, length) for axis, length in enumerate(array.shape)]
    main_axis = array.shape.index(max(array.shape))
    beside = index_at[:main_axis] + [(index_at[main_axis] + 1) % array.shape[main_axis]] + index_at[main_axis + 1:]
    return array.at[tuple(index_at)].set(least).at[tuple(beside)].set(top_value)


def levels(key, shape, cuts, smallest, high):
    level, own = 1.0, jax.random.fold_in(key, 6)
    for axis_at, shards_of in cuts:
        draws = jnp.exp(jax.random.uniform(jax.random.fold_in(own, axis_at), (shards_of,), jnp.float32, smallest / len(cuts), high / len(cuts)))
        level = level * jnp.repeat(draws, shape[axis_at] // shards_of).reshape([-1 if axis == axis_at else 1 for axis in range(len(shape))])
    return level


def scatter_about(stream_key, dims, spread, reach, cuts=(), held_as=jnp.bfloat16):
    gain = levels(stream_key, dims, cuts, -0.22, 0.18) if cuts else 1.0
    drawn = jax.random.normal(stream_key, dims, jnp.float32) * spread * gain
    return jnp.minimum(jnp.maximum(drawn, -reach), reach).astype(held_as)


def setup_inputs(seed: int = 0) -> dict:
    splits = jax.random.split(jax.random.key(seed), 10)
    events = scatter_about(splits[0], (SEQ, D), 1.0, 6.0, ((0, 768),))
    buckets = set_ends(jax.random.randint(splits[1], (SEQ,), 0, NB), jax.random.fold_in(splits[1], 1), 0, NB - 1).astype(jnp.int32)
    counts = draw_counts(jax.random.fold_in(splits[9], 71), 0)
    prior_keys = scatter_about(splits[3], (2 * BLOCK, D), 1.0, 6.0, ((1, 4),))
    prior_values = scatter_about(splits[4], (2 * BLOCK, D), 1.0, 6.0, ((1, 4),))
    prior_buckets = set_ends(jax.random.randint(splits[5], (2 * BLOCK,), 0, NB), jax.random.fold_in(splits[5], 1), 0, NB - 1).astype(jnp.int32)
    w_input = scatter_about(splits[6], (D, 4 * D), D ** -0.5, 0.1875)
    w_output = scatter_about(splits[7], (D, D), D ** -0.5, 0.1875)
    time_bias = scatter_about(splits[8], (NB, HEADS), 1.0, 4.0, (), jnp.float32)
    return {"events": events, "buckets": buckets, "counts": counts, "prior_keys": prior_keys, "prior_values": prior_values, "prior_buckets": prior_buckets, "w_input": w_input, "w_output": w_output, "time_bias": time_bias}


def layer_norm(values):
    mean = lax.optimization_barrier(jnp.mean(values, axis=-1, keepdims=True))
    centred = values - mean
    var = lax.optimization_barrier(jnp.mean(centred * centred, axis=-1, keepdims=True))
    return centred * lax.rsqrt(var + 1e-05)

def reference(events, buckets, counts, prior_keys, prior_values, prior_buckets, w_input, w_output, time_bias):
    normed = layer_norm(events.astype(jnp.float32)).astype(jnp.bfloat16)
    proj = jax.nn.silu(jnp.dot(normed, w_input, preferred_element_type=jnp.float32)).astype(jnp.bfloat16)
    gate_u = proj[:, 0:D]
    values = proj[:, D:2 * D]
    queries = proj[:, 2 * D:3 * D]
    keys = proj[:, 3 * D:4 * D]
    keys_pad = jnp.concatenate([prior_keys, keys], axis=0)
    values_pad = jnp.concatenate([prior_values, values], axis=0)
    buckets_pad = jnp.concatenate([prior_buckets.astype(jnp.int32), buckets.astype(jnp.int32)], axis=0)
    counts_pad = jnp.concatenate([jnp.full((2,), BLOCK, jnp.int32), counts.astype(jnp.int32)], axis=0)
    bias_table = time_bias.T
    rows = jnp.arange(BLOCK, dtype=jnp.int32)
    cols = jnp.arange(3 * BLOCK, dtype=jnp.int32)
    col_block = cols // BLOCK
    col_rest = cols % BLOCK

    def one_block(block):
        start = (block * BLOCK).astype(jnp.int32)
        query_rows = lax.dynamic_slice_in_dim(queries, start, BLOCK, 0).reshape(BLOCK, HEADS, HEAD_DIM)
        key_rows = lax.dynamic_slice_in_dim(keys_pad, start, 3 * BLOCK, 0).reshape(3 * BLOCK, HEADS, HEAD_DIM)
        value_rows = lax.dynamic_slice_in_dim(values_pad, start, 3 * BLOCK, 0).reshape(3 * BLOCK, HEADS, HEAD_DIM)
        query_buckets = lax.dynamic_slice_in_dim(buckets, start, BLOCK, 0).astype(jnp.int32)
        key_buckets = lax.dynamic_slice_in_dim(buckets_pad, start, 3 * BLOCK, 0)
        window_counts = lax.dynamic_slice_in_dim(counts_pad, block.astype(jnp.int32), 3, 0)
        key_count = lax.optimization_barrier(jnp.sum(jnp.where(col_block[:, None] == jnp.arange(3)[None, :], window_counts[None, :], 0), axis=1))
        valid = col_rest < key_count
        causal = (col_block[None, :] < 2) | (col_rest[None, :] <= rows[:, None])
        mask = valid[None, :] & causal
        scores = jnp.einsum('qhd,khd->hqk', query_rows.astype(jnp.float32), key_rows.astype(jnp.float32)) * 0.125
        distance = jnp.abs(query_buckets[:, None] - key_buckets[None, :])
        scores = scores + bias_table[:, distance]
        weight = jnp.where(mask[None, :, :], jax.nn.silu(scores), 0.0).astype(jnp.bfloat16)
        attended = jnp.einsum('hqk,khd->qhd', weight.astype(jnp.float32), value_rows.astype(jnp.float32))
        return attended.astype(jnp.bfloat16).reshape(BLOCK, D)
    attended = lax.map(one_block, jnp.arange(N_WIDE, dtype=jnp.int32)).reshape(SEQ, D)
    gated = (layer_norm(attended.astype(jnp.float32)) * gate_u.astype(jnp.float32)).astype(jnp.bfloat16)
    mixed = events.astype(jnp.float32) + jnp.dot(gated, w_output, preferred_element_type=jnp.float32)
    return mixed.astype(jnp.bfloat16)
```

```python
import jax
import jax.numpy as jnp
from jax import lax
from jax.experimental import pallas as pl
from jax.experimental.pallas import tpu as pltpu
from jax.sharding import Mesh, PartitionSpec as P


F32 = jnp.float32
BF16 = jnp.bfloat16
RING = ("side", "narrow")
ROWS = 128
LANES = 128
EXT = 136
NB = 64


def vmem():
    return pl.BlockSpec(memory_space=pltpu.VMEM)


def hbm():
    return pl.BlockSpec(memory_space=pltpu.HBM)


def limited(mib):
    return pltpu.CompilerParams(vmem_limit_bytes=mib << 20)


def cost(flops, moved):
    return pl.CostEstimate(flops=flops, bytes_accessed=moved, transcendentals=0)


def started(*copies):
    for copy in copies:
        copy.start()
    return copies


def silu_of_half(half):
    return half + half * jnp.tanh(half)


def standardised(values):
    mean = jnp.mean(values, axis=-1, keepdims=True)
    centred = values - mean
    var = jnp.mean(centred * centred, axis=-1, keepdims=True)
    return centred * lax.rsqrt(var + 1e-05)


STARTS = {"u": 0, "v": 1024, "q": 2048, "k": 3072}
ALL = 67_000_000


def weight_copies(w_hbm, ws, sems, kinds):
    width = ws.shape[2]
    return [
        pltpu.make_async_copy(w_hbm.at[:, pl.ds(STARTS[kind], width)], ws.at[i], sems.at[i])
        for i, kind in enumerate(kinds)
    ]


def place_parts(part, kind, n, place, valid, out_ref):
    lanes = slice(place * LANES, (place + 1) * LANES)
    if kind == "q":
        part = part * 0.0625
    if kind == "v":
        part = jnp.where(valid, part, 0.0)
    part = part.astype(BF16)
    out_ref[n, 0:ROWS, lanes] = part[:, 0:LANES]
    out_ref[4 + n, 0:ROWS, lanes] = part[:, LANES:]


def valid_rows(lag, counts):
    block = 2 * (lax.axis_index("outer") - lag) + lax.axis_index("side")
    count = counts[jnp.maximum(block, 0)]
    at = lax.broadcasted_iota(jnp.int32, (ROWS, 2 * LANES), 0)
    return at + lax.axis_index("narrow") * ROWS < count


def tail_rows(x_ref, out_ref):
    tail = x_ref[ROWS:EXT, 0 : out_ref.shape[2]]
    for s in range(8):
        out_ref[s, ROWS:EXT, :] = tail


def project_kernel(
    events_hbm, buckets_hbm, counts_hbm, w_hbm, normed_hbm, out_hbm, gate_hbm,
    events, buckets, counts, ws, normed, out, gate, in_sems, w_sems, out_sems
):
    small = started(
        pltpu.make_async_copy(events_hbm, events, in_sems.at[0]),
        pltpu.make_async_copy(buckets_hbm, buckets, in_sems.at[1]),
        pltpu.make_async_copy(counts_hbm, counts, in_sems.at[2]),
    )
    weights = started(*weight_copies(w_hbm, ws, w_sems, "qkvu"))
    for copy in small:
        copy.wait()
    x = standardised(events[...].astype(F32)).astype(BF16)
    normed[0:ROWS, :] = x
    own = buckets[pl.ds(lax.axis_index("narrow"), 1), :].astype(F32)
    width = normed.shape[1]
    row = jnp.concatenate([own] * (width // LANES), axis=1)
    normed[ROWS:EXT, :] = jnp.broadcast_to(row, (EXT - ROWS, width)).astype(BF16)
    sends = [pltpu.make_async_copy(normed, normed_hbm, out_sems.at[2])]
    sends[0].start()
    tail_rows(normed, out)
    valid = valid_rows(0, counts)
    for place, kind in enumerate("qkvu"):
        weights[place].wait()
        for n in range(4):
            lanes = slice(n * 2 * LANES, (n + 1) * 2 * LANES)
            w = ws[place, :, lanes]
            part = silu_of_half(0.5 * jnp.dot(x, w, preferred_element_type=F32))
            if kind == "u":
                gate[:, lanes] = part.astype(BF16)
            else:
                place_parts(part, kind, n, place, valid, out)
        if kind == "v":
            sends += started(pltpu.make_async_copy(out, out_hbm, out_sems.at[0]))
    sends += started(pltpu.make_async_copy(gate, gate_hbm, out_sems.at[1]))
    for copy in sends:
        copy.wait()


def project_call(events, buckets, counts, w_input):
    depth, width = w_input.shape
    return pl.pallas_call(
        project_kernel,
        out_shape=(
            jax.ShapeDtypeStruct((EXT, depth), BF16),
            jax.ShapeDtypeStruct((8, EXT, 3 * LANES), BF16),
            jax.ShapeDtypeStruct((ROWS, depth), BF16),
        ),
        in_specs=[hbm()] * 4,
        out_specs=(hbm(), hbm(), hbm()),
        scratch_shapes=[
            pltpu.VMEM((ROWS, depth), BF16),
            pltpu.VMEM((4, LANES), jnp.int32),
            pltpu.SMEM(counts.shape, jnp.int32),
            pltpu.VMEM((4, depth, 8 * LANES), BF16),
            pltpu.VMEM((EXT, depth), BF16),
            pltpu.VMEM((8, EXT, 3 * LANES), BF16),
            pltpu.VMEM((ROWS, depth), BF16),
            pltpu.SemaphoreType.DMA((3,)),
            pltpu.SemaphoreType.DMA((4,)),
            pltpu.SemaphoreType.DMA((3,)),
        ],
        cost_estimate=cost(2 * ROWS * depth * width, 2 * depth * width),
        compiler_params=pltpu.CompilerParams(vmem_limit_bytes=ALL),
        name="project_own",
    )(events, buckets, counts, w_input)


def project_prev_kernel(
    counts_hbm, x_hbm, w_hbm, out_hbm, counts, x, ws, out, in_sems, w_sems, out_sem
):
    small = started(
        pltpu.make_async_copy(x_hbm, x, in_sems.at[0]),
        pltpu.make_async_copy(counts_hbm, counts, in_sems.at[1]),
    )
    weights = started(*weight_copies(w_hbm, ws, w_sems, "kv"))
    for copy in small:
        copy.wait()
    valid = valid_rows(1, counts)
    tail_rows(x, out)
    for place, kind in enumerate("kv"):
        weights[place].wait()
        for n in range(4):
            w = ws[place, :, n * 2 * LANES : (n + 1) * 2 * LANES]
            dot = jnp.dot(x[0:ROWS, :], w, preferred_element_type=F32)
            place_parts(silu_of_half(0.5 * dot), kind, n, place, valid, out)
    send = pltpu.make_async_copy(out, out_hbm, out_sem)
    send.start()
    send.wait()


def project_prev_call(normed, counts, w_input):
    depth = w_input.shape[0]
    return pl.pallas_call(
        project_prev_kernel,
        out_shape=jax.ShapeDtypeStruct((8, EXT, 2 * LANES), BF16),
        in_specs=[hbm()] * 3,
        out_specs=hbm(),
        scratch_shapes=[
            pltpu.SMEM(counts.shape, jnp.int32),
            pltpu.VMEM((EXT, depth), BF16),
            pltpu.VMEM((2, depth, 8 * LANES), BF16),
            pltpu.VMEM((8, EXT, 2 * LANES), BF16),
            pltpu.SemaphoreType.DMA((2,)),
            pltpu.SemaphoreType.DMA((2,)),
            pltpu.SemaphoreType.DMA,
        ],
        cost_estimate=cost(4 * ROWS * depth * depth, 4 * depth * depth),
        compiler_params=pltpu.CompilerParams(vmem_limit_bytes=ALL),
        name="project_prev",
    )(counts, normed, w_input)


def hot_of(row):
    column = jnp.transpose(jnp.broadcast_to(row, (LANES, LANES)))
    lane = lax.broadcasted_iota(jnp.int32, (LANES, LANES), 1)
    wanted = jnp.where(lane >= NB, lane - NB, lane).astype(F32)
    return jnp.where(column == wanted, 1.0, 0.0).astype(BF16)


def bias_rows(bias_ref):
    at = lax.broadcasted_iota(jnp.int32, (NB, LANES), 1)
    gap = jnp.where(at <= NB, at, LANES - at)
    step = lax.broadcasted_iota(jnp.int32, (NB, LANES), 0)
    pick = jnp.where(gap == step, 1.0, 0.0).astype(F32)
    return 0.5 * lax.dot_general(
        bias_ref[...],
        pick,
        (((1,), (0,)), ((), ())),
        precision=lax.Precision.HIGHEST,
        preferred_element_type=F32,
    )


def pair_table(rows, head):
    at = lax.broadcasted_iota(jnp.int32, rows.shape, 0)
    row = jnp.sum(jnp.where(at == head, rows, 0.0), axis=0, keepdims=True)
    whole = jnp.broadcast_to(row, (NB, LANES))
    first = pltpu.roll(whole, 0, 1, stride=1, stride_axis=0)
    second = pltpu.roll(whole, NB, 1, stride=1, stride_axis=0)
    lane = lax.broadcasted_iota(jnp.int32, (NB, LANES), 1)
    coarse = first.astype(BF16)
    fine = (second - second.astype(BF16).astype(F32)).astype(BF16)
    table = jnp.where(lane < NB, coarse.astype(F32), fine.astype(F32))
    return jnp.concatenate([table, jnp.zeros_like(table)], axis=0).astype(BF16)


TILE = 256


def part_of(ref, start, size, place):
    s, n = start // LANES, size // LANES
    lanes = slice(place * LANES, (place + 1) * LANES)
    return ref[s : s + n, 0:ROWS, lanes].reshape(size, LANES)


def attended_sum(left, key, key_hot, value, ends=None):
    right = jnp.concatenate([key, key_hot], axis=1)
    half = lax.dot_general(left, right, (((1,), (1,)), ((), ())), preferred_element_type=F32)
    weight = silu_of_half(half)
    if ends is not None:
        r = lax.broadcasted_iota(jnp.int32, weight.shape, 0) + ends
        c = lax.broadcasted_iota(jnp.int32, weight.shape, 1)
        weight = jnp.where(c <= r, weight, 0.0)
    return jnp.dot(weight.astype(BF16), value, preferred_element_type=F32)


def attend_own_kernel(own_ref, bias_ref, left_ref, sum_ref, hot):
    for s in range(8):
        at = slice(s * LANES, (s + 1) * LANES)
        hot[at, :] = hot_of(own_ref[s, ROWS : ROWS + 1, 0:LANES].astype(F32))
    rows = bias_rows(bias_ref)
    head = lax.axis_index("narrow") * 4 + lax.axis_index("side") * 2
    tables = [pair_table(rows, head + j) for j in range(2)]
    lane = lax.broadcasted_iota(jnp.int32, (TILE, LANES), 1)
    halves = [lane < NB, lane >= NB]
    for b in range(2):
        for t in range(2):
            start = b * 512 + t * TILE
            at = slice(start, start + TILE)
            query = part_of(own_ref, start, TILE, 0).astype(F32)
            spans = [(0, 512, None)] if b == 1 else []
            if t == 1:
                spans.append((b * 512, TILE, None))
            spans.append((start, TILE, 0))
            sums = []
            for j in range(2):
                shifts = jnp.dot(hot[at, :], tables[j], preferred_element_type=F32).astype(BF16)
                mine = jnp.where(halves[j], query, 0.0).astype(BF16)
                left = jnp.concatenate([mine, shifts], axis=1)
                left_ref[j, at, :] = left
                total = None
                for first, size, ends in spans:
                    part = attended_sum(
                        left,
                        part_of(own_ref, first, size, 1),
                        hot[first : first + size, :],
                        part_of(own_ref, first, size, 2),
                        ends,
                    )
                    total = part if total is None else total + part
                sums.append(total)
            sum_ref[at, :] = jnp.where(halves[0], sums[0], sums[1])


def attend_own_call(own, bias_rows_in):
    return pl.pallas_call(
        attend_own_kernel,
        out_shape=(
            jax.ShapeDtypeStruct((2, 1024, 2 * LANES), BF16),
            jax.ShapeDtypeStruct((1024, LANES), F32),
        ),
        in_specs=[vmem(), vmem()],
        out_specs=(vmem(), vmem()),
        scratch_shapes=[pltpu.VMEM((1024, LANES), BF16)],
        cost_estimate=cost(2 * 1024 * 1024 * 512, 4 << 20),
        compiler_params=pltpu.CompilerParams(vmem_limit_bytes=ALL),
        name="attend_own",
    )(own, bias_rows_in)


def attend_prev_kernel(
    left_hbm, sum_hbm, prev_hbm, cache_k, cache_v, cache_b, out_hbm,
    left_ref, sum_ref, prev_ref, out_ref, keys, values, rows, hot, sems, in_sems, out_sems
):
    first = lax.axis_index("outer") == 0
    prev_copy, left_copy, sum_copy = started(
        pltpu.make_async_copy(prev_hbm, prev_ref, in_sems.at[0]),
        pltpu.make_async_copy(left_hbm, left_ref, in_sems.at[1]),
        pltpu.make_async_copy(sum_hbm, sum_ref, in_sems.at[2]),
    )
    prev_copy.wait()

    @pl.when(first)
    def _():
        start = pl.multiple_of(lax.axis_index("side") * LANES, LANES)
        copies = started(
            pltpu.make_async_copy(cache_k.at[:, pl.ds(start, LANES)], keys, sems.at[0]),
            pltpu.make_async_copy(cache_v.at[:, pl.ds(start, LANES)], values, sems.at[1]),
            pltpu.make_async_copy(cache_b, rows, sems.at[2]),
        )
        for copy in copies:
            copy.wait()

    @pl.when(jnp.logical_not(first))
    def _():
        for s in range(8):
            at = slice(s * LANES, (s + 1) * LANES)
            rows[s : s + 1, :] = prev_ref[s, ROWS : ROWS + 1, 0:LANES].astype(F32).astype(jnp.int32)
            keys[at, :] = prev_ref[s, 0:ROWS, 0:LANES]
            values[at, :] = prev_ref[s, 0:ROWS, LANES : 2 * LANES]

    for s in range(8):
        at = slice(s * LANES, (s + 1) * LANES)
        hot[at, :] = hot_of(rows[s : s + 1, :].astype(F32))
    left_copy.wait()
    sum_copy.wait()
    lane = lax.broadcasted_iota(jnp.int32, (TILE, LANES), 1)
    sends = []
    for b in range(2):
        for t in range(2):
            start = b * 512 + t * TILE
            at = slice(start, start + TILE)
            sums = []
            for j in range(2):
                total = None
                for begin in (0, 512) if b == 0 else (512,):
                    span = slice(begin, begin + 512)
                    part = attended_sum(left_ref[j, at, :], keys[span, :], hot[span, :], values[span, :])
                    total = part if total is None else total + part
                sums.append(total)
            whole = sum_ref[at, :] + jnp.where(lane < NB, sums[0], sums[1])
            s = start // LANES
            out_ref[s : s + 2, :, :] = whole.astype(BF16).reshape(2, LANES, LANES)
            two = pl.ds(s, 2)
            sends += started(
                pltpu.make_async_copy(out_ref.at[two], out_hbm.at[two], out_sems.at[s // 2])
            )
    for copy in sends:
        copy.wait()


def attend_prev_call(left, partial, prev, prior_keys, prior_values, prior_buckets):
    return pl.pallas_call(
        attend_prev_kernel,
        out_shape=jax.ShapeDtypeStruct((8, ROWS, LANES), BF16),
        in_specs=[hbm()] * 6,
        out_specs=hbm(),
        scratch_shapes=[
            pltpu.VMEM(left.shape, BF16),
            pltpu.VMEM(partial.shape, F32),
            pltpu.VMEM(prev.shape, BF16),
            pltpu.VMEM((8, ROWS, LANES), BF16),
            pltpu.VMEM((1024, LANES), BF16),
            pltpu.VMEM((1024, LANES), BF16),
            pltpu.VMEM((8, LANES), jnp.int32),
            pltpu.VMEM((1024, LANES), BF16),
            pltpu.SemaphoreType.DMA((3,)),
            pltpu.SemaphoreType.DMA((3,)),
            pltpu.SemaphoreType.DMA((4,)),
        ],
        cost_estimate=cost(4 * 1024 * 1024 * 1024, 4 << 20),
        compiler_params=pltpu.CompilerParams(vmem_limit_bytes=61 << 20),
        name="attend_prev",
    )(left, partial, prev, prior_keys, prior_values, prior_buckets)


def mix_kernel(attended_ref, gate_ref, events_ref, w_ref, out_ref):
    parts = [attended_ref[(c % 2) * 4 + c // 2] for c in range(8)]
    whole = jnp.concatenate(parts, axis=1).astype(F32)
    gated = (standardised(whole) * gate_ref[...].astype(F32)).astype(BF16)
    mixed = events_ref[...].astype(F32) + jnp.dot(
        gated, w_ref[...], preferred_element_type=F32
    )
    out_ref[...] = mixed.astype(BF16)


def mix_call(attended, gate, events, w_output):
    return pl.pallas_call(
        mix_kernel,
        out_shape=jax.ShapeDtypeStruct(events.shape, BF16),
        in_specs=[vmem(), vmem(), vmem(), vmem()],
        out_specs=vmem(),
        cost_estimate=cost(2 << 27, 3 << 20),
        compiler_params=limited(8),
        name="mix",
    )(attended, gate, events, w_output)


def exchanged(parts):
    return lax.all_to_all(parts, RING, split_axis=0, concat_axis=0, tiled=True)


def per_device(
    events, buckets, counts, prior_keys, prior_values, prior_buckets, w_input, w_output, time_bias
):
    outer = lax.axis_size("outer")
    normed, sent, gate = project_call(events, buckets.reshape(4, LANES), counts, w_input)
    earlier = lax.ppermute(normed, "outer", [(i, i + 1) for i in range(outer - 1)])
    own = exchanged(sent)
    sent = project_prev_call(earlier, counts, w_input)
    prev = exchanged(sent)
    left, partial = attend_own_call(own, time_bias.T)
    attended = attend_prev_call(
        left, partial, prev, prior_keys, prior_values, prior_buckets.reshape(8, LANES)
    )
    attended = exchanged(attended)
    return mix_call(attended, gate, events, w_output)


def solution(mesh):
    rings = Mesh(
        mesh.devices.reshape(mesh.devices.shape[0] // 2, 2, mesh.devices.shape[1]),
        ("outer", "side", "narrow"),
    )
    placed = (
        P(("outer", "side", "narrow"), None),
        P(("outer", "side")),
        P(),
        P(None, "narrow"),
        P(None, "narrow"),
        P(),
        P(),
        P(),
        P(),
    )
    return jax.shard_map(
        per_device,
        mesh=rings,
        in_specs=placed,
        out_specs=P(("outer", "side", "narrow"), None),
        check_vma=False,
    )
```

```python
import jax
import jax.numpy as jnp
from jax import lax
from jax.experimental import pallas as pl
from jax.experimental.pallas import tpu as pltpu
from jax.sharding import Mesh, PartitionSpec as P


F32 = jnp.float32
BF16 = jnp.bfloat16
RING = ("side", "narrow")
ROWS = 128
LANES = 128
EXT = 136
NB = 64


def vmem():
    return pl.BlockSpec(memory_space=pltpu.VMEM)


def hbm():
    return pl.BlockSpec(memory_space=pltpu.HBM)


def limited(mib):
    return pltpu.CompilerParams(vmem_limit_bytes=mib << 20)


def cost(flops, moved):
    return pl.CostEstimate(flops=flops, bytes_accessed=moved, transcendentals=0)


def started(*copies):
    for copy in copies:
        copy.start()
    return copies


def silu_of_half(half):
    return half + half * jnp.tanh(half)


def standardised(values):
    mean = jnp.mean(values, axis=-1, keepdims=True)
    centred = values - mean
    var = jnp.mean(centred * centred, axis=-1, keepdims=True)
    return centred * lax.rsqrt(var + 1e-05)


STARTS = {"u": 0, "v": 1024, "q": 2048, "k": 3072}
ALL = 67_000_000


def weight_copies(w_hbm, ws, sems, kinds):
    width = ws.shape[2]
    return [
        pltpu.make_async_copy(w_hbm.at[:, pl.ds(STARTS[kind], width)], ws.at[i], sems.at[i])
        for i, kind in enumerate(kinds)
    ]


def place_parts(part, kind, n, place, valid, out_ref):
    lanes = slice(place * LANES, (place + 1) * LANES)
    if kind == "q":
        part = part * 0.0625
    if kind == "v":
        part = jnp.where(valid, part, 0.0)
    part = part.astype(BF16)
    out_ref[n, 0:ROWS, lanes] = part[:, 0:LANES]
    out_ref[4 + n, 0:ROWS, lanes] = part[:, LANES:]


def valid_rows(lag, counts):
    block = 2 * (lax.axis_index("outer") - lag) + lax.axis_index("side")
    count = counts[jnp.maximum(block, 0)]
    at = lax.broadcasted_iota(jnp.int32, (ROWS, 2 * LANES), 0)
    return at + lax.axis_index("narrow") * ROWS < count


def tail_rows(x_ref, out_ref):
    tail = x_ref[ROWS:EXT, 0 : out_ref.shape[2]]
    for s in range(8):
        out_ref[s, ROWS:EXT, :] = tail


def project_kernel(
    events_hbm, buckets_hbm, counts_hbm, w_hbm, normed_hbm, out_hbm,
    events, buckets, counts, ws, normed, out, in_sems, w_sems, out_sems
):
    small = started(
        pltpu.make_async_copy(events_hbm, events, in_sems.at[0]),
        pltpu.make_async_copy(buckets_hbm, buckets, in_sems.at[1]),
        pltpu.make_async_copy(counts_hbm, counts, in_sems.at[2]),
    )
    weights = started(*weight_copies(w_hbm, ws, w_sems, "qkv"))
    for copy in small:
        copy.wait()
    x = standardised(events[...].astype(F32)).astype(BF16)
    normed[0:ROWS, :] = x
    own = buckets[pl.ds(lax.axis_index("narrow"), 1), :].astype(F32)
    width = normed.shape[1]
    row = jnp.concatenate([own] * (width // LANES), axis=1)
    normed[ROWS:EXT, :] = jnp.broadcast_to(row, (EXT - ROWS, width)).astype(BF16)
    sends = [pltpu.make_async_copy(normed, normed_hbm, out_sems.at[3])]
    sends[0].start()
    tail_rows(normed, out)
    valid = valid_rows(0, counts)
    for place, kind in enumerate("qkv"):
        weights[place].wait()
        for n in range(4):
            w = ws[place, :, n * 2 * LANES : (n + 1) * 2 * LANES]
            part = silu_of_half(0.5 * jnp.dot(x, w, preferred_element_type=F32))
            place_parts(part, kind, n, place, valid, out)
        lanes = pl.ds(place * LANES, LANES)
        sends += started(
            pltpu.make_async_copy(out.at[:, :, lanes], out_hbm.at[:, :, lanes], out_sems.at[place])
        )
    for copy in sends:
        copy.wait()


def project_call(events, buckets, counts, w_input):
    depth, width = w_input.shape
    return pl.pallas_call(
        project_kernel,
        out_shape=(
            jax.ShapeDtypeStruct((EXT, depth), BF16),
            jax.ShapeDtypeStruct((8, EXT, 3 * LANES), BF16),
        ),
        in_specs=[hbm()] * 4,
        out_specs=(hbm(), hbm()),
        scratch_shapes=[
            pltpu.VMEM((ROWS, depth), BF16),
            pltpu.VMEM((4, LANES), jnp.int32),
            pltpu.SMEM(counts.shape, jnp.int32),
            pltpu.VMEM((3, depth, 8 * LANES), BF16),
            pltpu.VMEM((EXT, depth), BF16),
            pltpu.VMEM((8, EXT, 3 * LANES), BF16),
            pltpu.SemaphoreType.DMA((3,)),
            pltpu.SemaphoreType.DMA((3,)),
            pltpu.SemaphoreType.DMA((4,)),
        ],
        cost_estimate=cost(2 * ROWS * depth * width, 2 * depth * width),
        compiler_params=pltpu.CompilerParams(vmem_limit_bytes=ALL),
        name="project_own",
    )(events, buckets, counts, w_input)


def project_prev_kernel(
    counts_hbm, x_hbm, w_hbm, out_hbm, counts, x, ws, out, in_sems, w_sems, out_sem
):
    small = started(
        pltpu.make_async_copy(x_hbm, x, in_sems.at[0]),
        pltpu.make_async_copy(counts_hbm, counts, in_sems.at[1]),
    )
    weights = started(*weight_copies(w_hbm, ws, w_sems, "kv"))
    for copy in small:
        copy.wait()
    valid = valid_rows(1, counts)
    tail_rows(x, out)
    for place, kind in enumerate("kv"):
        weights[place].wait()
        for n in range(4):
            w = ws[place, :, n * 2 * LANES : (n + 1) * 2 * LANES]
            dot = jnp.dot(x[0:ROWS, :], w, preferred_element_type=F32)
            place_parts(silu_of_half(0.5 * dot), kind, n, place, valid, out)
    send = pltpu.make_async_copy(out, out_hbm, out_sem)
    send.start()
    send.wait()


def project_prev_call(normed, counts, w_input):
    depth = w_input.shape[0]
    return pl.pallas_call(
        project_prev_kernel,
        out_shape=jax.ShapeDtypeStruct((8, EXT, 2 * LANES), BF16),
        in_specs=[hbm()] * 3,
        out_specs=hbm(),
        scratch_shapes=[
            pltpu.SMEM(counts.shape, jnp.int32),
            pltpu.VMEM((EXT, depth), BF16),
            pltpu.VMEM((2, depth, 8 * LANES), BF16),
            pltpu.VMEM((8, EXT, 2 * LANES), BF16),
            pltpu.SemaphoreType.DMA((2,)),
            pltpu.SemaphoreType.DMA((2,)),
            pltpu.SemaphoreType.DMA,
        ],
        cost_estimate=cost(4 * ROWS * depth * depth, 4 * depth * depth),
        compiler_params=pltpu.CompilerParams(vmem_limit_bytes=ALL),
        name="project_prev",
    )(counts, normed, w_input)


def gate_kernel(x_hbm, w_hbm, out_ref, x, ws, sems):
    copies = started(
        pltpu.make_async_copy(x_hbm, x, sems.at[0]),
        pltpu.make_async_copy(w_hbm.at[:, pl.ds(STARTS["u"], ws.shape[1])], ws, sems.at[1]),
    )
    for copy in copies:
        copy.wait()
    for n in range(4):
        lanes = slice(n * 2 * LANES, (n + 1) * 2 * LANES)
        half = 0.5 * jnp.dot(x[0:ROWS, :], ws[:, lanes], preferred_element_type=F32)
        out_ref[:, lanes] = silu_of_half(half).astype(BF16)


def gate_call(normed, w_input):
    depth = w_input.shape[0]
    return pl.pallas_call(
        gate_kernel,
        out_shape=jax.ShapeDtypeStruct((ROWS, depth), BF16),
        in_specs=[hbm(), hbm()],
        out_specs=vmem(),
        scratch_shapes=[
            pltpu.VMEM((EXT, depth), BF16),
            pltpu.VMEM((depth, depth), BF16),
            pltpu.SemaphoreType.DMA((2,)),
        ],
        cost_estimate=cost(2 * ROWS * depth * depth, 2 * depth * depth),
        compiler_params=pltpu.CompilerParams(vmem_limit_bytes=ALL),
        name="project_u",
    )(normed, w_input)


def hot_of(row):
    column = jnp.transpose(jnp.broadcast_to(row, (LANES, LANES)))
    lane = lax.broadcasted_iota(jnp.int32, (LANES, LANES), 1)
    wanted = jnp.where(lane >= NB, lane - NB, lane).astype(F32)
    return jnp.where(column == wanted, 1.0, 0.0).astype(BF16)


def bias_rows(bias_ref):
    at = lax.broadcasted_iota(jnp.int32, (NB, LANES), 1)
    gap = jnp.where(at <= NB, at, LANES - at)
    step = lax.broadcasted_iota(jnp.int32, (NB, LANES), 0)
    pick = jnp.where(gap == step, 1.0, 0.0).astype(F32)
    return 0.5 * lax.dot_general(
        bias_ref[...],
        pick,
        (((1,), (0,)), ((), ())),
        precision=lax.Precision.HIGHEST,
        preferred_element_type=F32,
    )


def pair_table(rows, head):
    at = lax.broadcasted_iota(jnp.int32, rows.shape, 0)
    row = jnp.sum(jnp.where(at == head, rows, 0.0), axis=0, keepdims=True)
    whole = jnp.broadcast_to(row, (NB, LANES))
    first = pltpu.roll(whole, 0, 1, stride=1, stride_axis=0)
    second = pltpu.roll(whole, NB, 1, stride=1, stride_axis=0)
    lane = lax.broadcasted_iota(jnp.int32, (NB, LANES), 1)
    coarse = first.astype(BF16)
    fine = (second - second.astype(BF16).astype(F32)).astype(BF16)
    table = jnp.where(lane < NB, coarse.astype(F32), fine.astype(F32))
    return jnp.concatenate([table, jnp.zeros_like(table)], axis=0).astype(BF16)


TILE = 256


def part_of(ref, start, size, place):
    s, n = start // LANES, size // LANES
    lanes = slice(place * LANES, (place + 1) * LANES)
    return ref[s : s + n, 0:ROWS, lanes].reshape(size, LANES)


def attended_sum(left, key, key_hot, value, ends=None):
    right = jnp.concatenate([key, key_hot], axis=1)
    half = lax.dot_general(left, right, (((1,), (1,)), ((), ())), preferred_element_type=F32)
    weight = silu_of_half(half)
    if ends is not None:
        r = lax.broadcasted_iota(jnp.int32, weight.shape, 0) + ends
        c = lax.broadcasted_iota(jnp.int32, weight.shape, 1)
        weight = jnp.where(c <= r, weight, 0.0)
    return jnp.dot(weight.astype(BF16), value, preferred_element_type=F32)


def attend_own_kernel(own_ref, bias_ref, left_ref, sum_ref, hot):
    for s in range(8):
        at = slice(s * LANES, (s + 1) * LANES)
        hot[at, :] = hot_of(own_ref[s, ROWS : ROWS + 1, 0:LANES].astype(F32))
    rows = bias_rows(bias_ref)
    head = lax.axis_index("narrow") * 4 + lax.axis_index("side") * 2
    tables = [pair_table(rows, head + j) for j in range(2)]
    lane = lax.broadcasted_iota(jnp.int32, (TILE, LANES), 1)
    halves = [lane < NB, lane >= NB]
    for b in range(2):
        for t in range(2):
            start = b * 512 + t * TILE
            at = slice(start, start + TILE)
            query = part_of(own_ref, start, TILE, 0).astype(F32)
            spans = [(0, 512, None)] if b == 1 else []
            if t == 1:
                spans.append((b * 512, TILE, None))
            spans.append((start, TILE, 0))
            sums = []
            for j in range(2):
                shifts = jnp.dot(hot[at, :], tables[j], preferred_element_type=F32).astype(BF16)
                mine = jnp.where(halves[j], query, 0.0).astype(BF16)
                left = jnp.concatenate([mine, shifts], axis=1)
                left_ref[j, at, :] = left
                total = None
                for first, size, ends in spans:
                    part = attended_sum(
                        left,
                        part_of(own_ref, first, size, 1),
                        hot[first : first + size, :],
                        part_of(own_ref, first, size, 2),
                        ends,
                    )
                    total = part if total is None else total + part
                sums.append(total)
            sum_ref[at, :] = jnp.where(halves[0], sums[0], sums[1])


def attend_own_call(own, bias_rows_in):
    return pl.pallas_call(
        attend_own_kernel,
        out_shape=(
            jax.ShapeDtypeStruct((2, 1024, 2 * LANES), BF16),
            jax.ShapeDtypeStruct((1024, LANES), F32),
        ),
        in_specs=[vmem(), vmem()],
        out_specs=(vmem(), vmem()),
        scratch_shapes=[pltpu.VMEM((1024, LANES), BF16)],
        cost_estimate=cost(2 * 1024 * 1024 * 512, 4 << 20),
        compiler_params=pltpu.CompilerParams(vmem_limit_bytes=ALL),
        name="attend_own",
    )(own, bias_rows_in)


def attend_prev_kernel(
    left_hbm, sum_hbm, prev_hbm, cache_k, cache_v, cache_b, out_hbm,
    left_ref, sum_ref, prev_ref, out_ref, keys, values, rows, hot, sems, in_sems, out_sems
):
    first = lax.axis_index("outer") == 0
    prev_copy, left_copy, sum_copy = started(
        pltpu.make_async_copy(prev_hbm, prev_ref, in_sems.at[0]),
        pltpu.make_async_copy(left_hbm, left_ref, in_sems.at[1]),
        pltpu.make_async_copy(sum_hbm, sum_ref, in_sems.at[2]),
    )
    prev_copy.wait()

    @pl.when(first)
    def _():
        start = pl.multiple_of(lax.axis_index("side") * LANES, LANES)
        copies = started(
            pltpu.make_async_copy(cache_k.at[:, pl.ds(start, LANES)], keys, sems.at[0]),
            pltpu.make_async_copy(cache_v.at[:, pl.ds(start, LANES)], values, sems.at[1]),
            pltpu.make_async_copy(cache_b, rows, sems.at[2]),
        )
        for copy in copies:
            copy.wait()

    @pl.when(jnp.logical_not(first))
    def _():
        for s in range(8):
            at = slice(s * LANES, (s + 1) * LANES)
            rows[s : s + 1, :] = prev_ref[s, ROWS : ROWS + 1, 0:LANES].astype(F32).astype(jnp.int32)
            keys[at, :] = prev_ref[s, 0:ROWS, 0:LANES]
            values[at, :] = prev_ref[s, 0:ROWS, LANES : 2 * LANES]

    for s in range(8):
        at = slice(s * LANES, (s + 1) * LANES)
        hot[at, :] = hot_of(rows[s : s + 1, :].astype(F32))
    left_copy.wait()
    sum_copy.wait()
    lane = lax.broadcasted_iota(jnp.int32, (TILE, LANES), 1)
    sends = []
    for b in range(2):
        for t in range(2):
            start = b * 512 + t * TILE
            at = slice(start, start + TILE)
            sums = []
            for j in range(2):
                total = None
                for begin in (0, 512) if b == 0 else (512,):
                    span = slice(begin, begin + 512)
                    part = attended_sum(left_ref[j, at, :], keys[span, :], hot[span, :], values[span, :])
                    total = part if total is None else total + part
                sums.append(total)
            whole = sum_ref[at, :] + jnp.where(lane < NB, sums[0], sums[1])
            s = start // LANES
            out_ref[s : s + 2, :, :] = whole.astype(BF16).reshape(2, LANES, LANES)
            two = pl.ds(s, 2)
            sends += started(
                pltpu.make_async_copy(out_ref.at[two], out_hbm.at[two], out_sems.at[s // 2])
            )
    for copy in sends:
        copy.wait()


def attend_prev_call(left, partial, prev, prior_keys, prior_values, prior_buckets):
    return pl.pallas_call(
        attend_prev_kernel,
        out_shape=jax.ShapeDtypeStruct((8, ROWS, LANES), BF16),
        in_specs=[hbm()] * 6,
        out_specs=hbm(),
        scratch_shapes=[
            pltpu.VMEM(left.shape, BF16),
            pltpu.VMEM(partial.shape, F32),
            pltpu.VMEM(prev.shape, BF16),
            pltpu.VMEM((8, ROWS, LANES), BF16),
            pltpu.VMEM((1024, LANES), BF16),
            pltpu.VMEM((1024, LANES), BF16),
            pltpu.VMEM((8, LANES), jnp.int32),
            pltpu.VMEM((1024, LANES), BF16),
            pltpu.SemaphoreType.DMA((3,)),
            pltpu.SemaphoreType.DMA((3,)),
            pltpu.SemaphoreType.DMA((4,)),
        ],
        cost_estimate=cost(4 * 1024 * 1024 * 1024, 4 << 20),
        compiler_params=pltpu.CompilerParams(vmem_limit_bytes=61 << 20),
        name="attend_prev",
    )(left, partial, prev, prior_keys, prior_values, prior_buckets)


def mix_kernel(attended_ref, gate_ref, events_ref, w_ref, out_ref):
    parts = [attended_ref[(c % 2) * 4 + c // 2] for c in range(8)]
    whole = jnp.concatenate(parts, axis=1).astype(F32)
    gated = (standardised(whole) * gate_ref[...].astype(F32)).astype(BF16)
    mixed = events_ref[...].astype(F32) + jnp.dot(
        gated, w_ref[...], preferred_element_type=F32
    )
    out_ref[...] = mixed.astype(BF16)


def mix_call(attended, gate, events, w_output):
    return pl.pallas_call(
        mix_kernel,
        out_shape=jax.ShapeDtypeStruct(events.shape, BF16),
        in_specs=[vmem(), vmem(), vmem(), vmem()],
        out_specs=vmem(),
        cost_estimate=cost(2 << 27, 3 << 20),
        compiler_params=limited(8),
        name="mix",
    )(attended, gate, events, w_output)


def exchanged(parts):
    return lax.all_to_all(parts, RING, split_axis=0, concat_axis=0, tiled=True)


def per_device(
    events, buckets, counts, prior_keys, prior_values, prior_buckets, w_input, w_output, time_bias
):
    outer = lax.axis_size("outer")
    normed, sent = project_call(events, buckets.reshape(4, LANES), counts, w_input)
    earlier = lax.ppermute(normed, "outer", [(i, i + 1) for i in range(outer - 1)])
    own = exchanged(sent)
    gate = gate_call(normed, w_input)
    sent = project_prev_call(earlier, counts, w_input)
    prev = exchanged(sent)
    left, partial = attend_own_call(own, time_bias.T)
    attended = attend_prev_call(
        left, partial, prev, prior_keys, prior_values, prior_buckets.reshape(8, LANES)
    )
    attended = exchanged(attended)
    return mix_call(attended, gate, events, w_output)


def solution(mesh):
    rings = Mesh(
        mesh.devices.reshape(mesh.devices.shape[0] // 2, 2, mesh.devices.shape[1]),
        ("outer", "side", "narrow"),
    )
    placed = (
        P(("outer", "side", "narrow"), None),
        P(("outer", "side")),
        P(),
        P(None, "narrow"),
        P(None, "narrow"),
        P(),
        P(),
        P(),
        P(),
    )
    return jax.shard_map(
        per_device,
        mesh=rings,
        in_specs=placed,
        out_specs=P(("outer", "side", "narrow"), None),
        check_vma=False,
    )
```

```python
import jax
import jax.numpy as jnp
from jax import lax
from jax.experimental import pallas as pl
from jax.experimental.pallas import tpu as pltpu
from jax.sharding import Mesh, PartitionSpec as P


F32 = jnp.float32
BF16 = jnp.bfloat16
RING = ("side", "narrow")
ROWS = 128
LANES = 128
EXT = 136
NB = 64


def vmem():
    return pl.BlockSpec(memory_space=pltpu.VMEM)


def hbm():
    return pl.BlockSpec(memory_space=pltpu.HBM)


def limited(mib):
    return pltpu.CompilerParams(vmem_limit_bytes=mib << 20)


def cost(flops, moved):
    return pl.CostEstimate(flops=flops, bytes_accessed=moved, transcendentals=0)


def started(*copies):
    for copy in copies:
        copy.start()
    return copies


def silu_of_half(half):
    return half + half * jnp.tanh(half)


def standardised(values):
    mean = jnp.mean(values, axis=-1, keepdims=True)
    centred = values - mean
    var = jnp.mean(centred * centred, axis=-1, keepdims=True)
    return centred * lax.rsqrt(var + 1e-05)


STARTS = {"u": 0, "v": 1024, "q": 2048, "k": 3072}
ALL = 67_000_000


def weight_copies(w_hbm, ws, sems, kinds):
    width = ws.shape[2]
    return [
        pltpu.make_async_copy(w_hbm.at[:, pl.ds(STARTS[kind], width)], ws.at[i], sems.at[i])
        for i, kind in enumerate(kinds)
    ]


def place_parts(part, kind, n, place, valid, out_ref):
    lanes = slice(place * LANES, (place + 1) * LANES)
    if kind == "q":
        part = part * 0.0625
    if kind == "v":
        part = jnp.where(valid, part, 0.0)
    part = part.astype(BF16)
    out_ref[n, 0:ROWS, lanes] = part[:, 0:LANES]
    out_ref[4 + n, 0:ROWS, lanes] = part[:, LANES:]


def valid_rows(lag, counts):
    block = 2 * (lax.axis_index("outer") - lag) + lax.axis_index("side")
    count = counts[jnp.maximum(block, 0)]
    at = lax.broadcasted_iota(jnp.int32, (ROWS, 2 * LANES), 0)
    return at + lax.axis_index("narrow") * ROWS < count


def tail_rows(x_ref, out_ref):
    tail = x_ref[ROWS:EXT, 0 : out_ref.shape[2]]
    for s in range(8):
        out_ref[s, ROWS:EXT, :] = tail


def project_kernel(
    events_hbm, buckets_hbm, counts_hbm, w_hbm, normed_hbm, out_hbm,
    events, buckets, counts, ws, normed, out, in_sems, w_sems, out_sems
):
    small = started(
        pltpu.make_async_copy(events_hbm, events, in_sems.at[0]),
        pltpu.make_async_copy(buckets_hbm, buckets, in_sems.at[1]),
        pltpu.make_async_copy(counts_hbm, counts, in_sems.at[2]),
    )
    weights = started(*weight_copies(w_hbm, ws, w_sems, "qkv"))
    for copy in small:
        copy.wait()
    x = standardised(events[...].astype(F32)).astype(BF16)
    normed[0:ROWS, :] = x
    own = buckets[pl.ds(lax.axis_index("narrow"), 1), :].astype(F32)
    width = normed.shape[1]
    row = jnp.concatenate([own] * (width // LANES), axis=1)
    normed[ROWS:EXT, :] = jnp.broadcast_to(row, (EXT - ROWS, width)).astype(BF16)
    sends = [pltpu.make_async_copy(normed, normed_hbm, out_sems.at[3])]
    sends[0].start()
    tail_rows(normed, out)
    valid = valid_rows(0, counts)
    for place, kind in enumerate("qkv"):
        weights[place].wait()
        for n in range(4):
            w = ws[place, :, n * 2 * LANES : (n + 1) * 2 * LANES]
            part = silu_of_half(0.5 * jnp.dot(x, w, preferred_element_type=F32))
            place_parts(part, kind, n, place, valid, out)
        lanes = pl.ds(place * LANES, LANES)
        sends += started(
            pltpu.make_async_copy(out.at[:, :, lanes], out_hbm.at[:, :, lanes], out_sems.at[place])
        )
    for copy in sends:
        copy.wait()


def project_call(events, buckets, counts, w_input):
    depth, width = w_input.shape
    return pl.pallas_call(
        project_kernel,
        out_shape=(
            jax.ShapeDtypeStruct((EXT, depth), BF16),
            jax.ShapeDtypeStruct((8, EXT, 3 * LANES), BF16),
        ),
        in_specs=[hbm()] * 4,
        out_specs=(hbm(), hbm()),
        scratch_shapes=[
            pltpu.VMEM((ROWS, depth), BF16),
            pltpu.VMEM((4, LANES), jnp.int32),
            pltpu.SMEM(counts.shape, jnp.int32),
            pltpu.VMEM((3, depth, 8 * LANES), BF16),
            pltpu.VMEM((EXT, depth), BF16),
            pltpu.VMEM((8, EXT, 3 * LANES), BF16),
            pltpu.SemaphoreType.DMA((3,)),
            pltpu.SemaphoreType.DMA((3,)),
            pltpu.SemaphoreType.DMA((4,)),
        ],
        cost_estimate=cost(2 * ROWS * depth * width, 2 * depth * width),
        compiler_params=pltpu.CompilerParams(vmem_limit_bytes=ALL),
        name="project_own",
    )(events, buckets, counts, w_input)


def project_prev_kernel(
    counts_hbm, x_hbm, w_hbm, out_hbm, counts, x, ws, out, in_sems, w_sems, out_sem
):
    small = started(
        pltpu.make_async_copy(x_hbm, x, in_sems.at[0]),
        pltpu.make_async_copy(counts_hbm, counts, in_sems.at[1]),
    )
    weights = started(*weight_copies(w_hbm, ws, w_sems, "kv"))
    for copy in small:
        copy.wait()
    valid = valid_rows(1, counts)
    tail_rows(x, out)
    for place, kind in enumerate("kv"):
        weights[place].wait()
        for n in range(4):
            w = ws[place, :, n * 2 * LANES : (n + 1) * 2 * LANES]
            dot = jnp.dot(x[0:ROWS, :], w, preferred_element_type=F32)
            place_parts(silu_of_half(0.5 * dot), kind, n, place, valid, out)
    send = pltpu.make_async_copy(out, out_hbm, out_sem)
    send.start()
    send.wait()


def project_prev_call(normed, counts, w_input):
    depth = w_input.shape[0]
    return pl.pallas_call(
        project_prev_kernel,
        out_shape=jax.ShapeDtypeStruct((8, EXT, 2 * LANES), BF16),
        in_specs=[hbm()] * 3,
        out_specs=hbm(),
        scratch_shapes=[
            pltpu.SMEM(counts.shape, jnp.int32),
            pltpu.VMEM((EXT, depth), BF16),
            pltpu.VMEM((2, depth, 8 * LANES), BF16),
            pltpu.VMEM((8, EXT, 2 * LANES), BF16),
            pltpu.SemaphoreType.DMA((2,)),
            pltpu.SemaphoreType.DMA((2,)),
            pltpu.SemaphoreType.DMA,
        ],
        cost_estimate=cost(4 * ROWS * depth * depth, 4 * depth * depth),
        compiler_params=pltpu.CompilerParams(vmem_limit_bytes=ALL),
        name="project_prev",
    )(counts, normed, w_input)


def gate_kernel(x_hbm, w_hbm, out_ref, x, ws, sems):
    copies = started(
        pltpu.make_async_copy(x_hbm, x, sems.at[0]),
        pltpu.make_async_copy(w_hbm.at[:, pl.ds(STARTS["u"], ws.shape[1])], ws, sems.at[1]),
    )
    for copy in copies:
        copy.wait()
    for n in range(4):
        lanes = slice(n * 2 * LANES, (n + 1) * 2 * LANES)
        half = 0.5 * jnp.dot(x[0:ROWS, :], ws[:, lanes], preferred_element_type=F32)
        out_ref[:, lanes] = silu_of_half(half).astype(BF16)


def gate_call(normed, w_input):
    depth = w_input.shape[0]
    return pl.pallas_call(
        gate_kernel,
        out_shape=jax.ShapeDtypeStruct((ROWS, depth), BF16),
        in_specs=[hbm(), hbm()],
        out_specs=vmem(),
        scratch_shapes=[
            pltpu.VMEM((EXT, depth), BF16),
            pltpu.VMEM((depth, depth), BF16),
            pltpu.SemaphoreType.DMA((2,)),
        ],
        cost_estimate=cost(2 * ROWS * depth * depth, 2 * depth * depth),
        compiler_params=pltpu.CompilerParams(vmem_limit_bytes=ALL),
        name="project_u",
    )(normed, w_input)


def hot_of(row):
    column = jnp.transpose(jnp.broadcast_to(row, (LANES, LANES)))
    lane = lax.broadcasted_iota(jnp.int32, (LANES, LANES), 1)
    wanted = jnp.where(lane >= NB, lane - NB, lane).astype(F32)
    return jnp.where(column == wanted, 1.0, 0.0).astype(BF16)


def bias_rows(bias_ref):
    at = lax.broadcasted_iota(jnp.int32, (NB, LANES), 1)
    gap = jnp.where(at <= NB, at, LANES - at)
    step = lax.broadcasted_iota(jnp.int32, (NB, LANES), 0)
    pick = jnp.where(gap == step, 1.0, 0.0).astype(F32)
    return 0.5 * lax.dot_general(
        bias_ref[...],
        pick,
        (((1,), (0,)), ((), ())),
        precision=lax.Precision.HIGHEST,
        preferred_element_type=F32,
    )


def pair_table(rows, head):
    at = lax.broadcasted_iota(jnp.int32, rows.shape, 0)
    row = jnp.sum(jnp.where(at == head, rows, 0.0), axis=0, keepdims=True)
    whole = jnp.broadcast_to(row, (NB, LANES))
    first = pltpu.roll(whole, 0, 1, stride=1, stride_axis=0)
    second = pltpu.roll(whole, NB, 1, stride=1, stride_axis=0)
    lane = lax.broadcasted_iota(jnp.int32, (NB, LANES), 1)
    coarse = first.astype(BF16)
    fine = (second - second.astype(BF16).astype(F32)).astype(BF16)
    table = jnp.where(lane < NB, coarse.astype(F32), fine.astype(F32))
    return jnp.concatenate([table, jnp.zeros_like(table)], axis=0).astype(BF16)


TILE = 256


def part_of(ref, start, size, place):
    s, n = start // LANES, size // LANES
    lanes = slice(place * LANES, (place + 1) * LANES)
    return ref[s : s + n, 0:ROWS, lanes].reshape(size, LANES)


def attended_sum(left, key, key_hot, value, ends=None):
    right = jnp.concatenate([key, key_hot], axis=1)
    half = lax.dot_general(left, right, (((1,), (1,)), ((), ())), preferred_element_type=F32)
    weight = silu_of_half(half)
    if ends is not None:
        r = lax.broadcasted_iota(jnp.int32, weight.shape, 0) + ends
        c = lax.broadcasted_iota(jnp.int32, weight.shape, 1)
        weight = jnp.where(c <= r, weight, 0.0)
    return jnp.dot(weight.astype(BF16), value, preferred_element_type=F32)


def attend_own_kernel(own_ref, bias_ref, left_ref, sum_ref, hot):
    for s in range(8):
        at = slice(s * LANES, (s + 1) * LANES)
        hot[at, :] = hot_of(own_ref[s, ROWS : ROWS + 1, 0:LANES].astype(F32))
    rows = bias_rows(bias_ref)
    head = lax.axis_index("narrow") * 4 + lax.axis_index("side") * 2
    tables = [pair_table(rows, head + j) for j in range(2)]
    lane = lax.broadcasted_iota(jnp.int32, (TILE, LANES), 1)
    halves = [lane < NB, lane >= NB]
    for b in range(2):
        for t in range(2):
            start = b * 512 + t * TILE
            at = slice(start, start + TILE)
            query = part_of(own_ref, start, TILE, 0).astype(F32)
            spans = [(0, 512, None)] if b == 1 else []
            if t == 1:
                spans.append((b * 512, TILE, None))
            spans.append((start, TILE, 0))
            sums = []
            for j in range(2):
                shifts = jnp.dot(hot[at, :], tables[j], preferred_element_type=F32).astype(BF16)
                mine = jnp.where(halves[j], query, 0.0).astype(BF16)
                left = jnp.concatenate([mine, shifts], axis=1)
                left_ref[j, at, :] = left
                total = None
                for first, size, ends in spans:
                    part = attended_sum(
                        left,
                        part_of(own_ref, first, size, 1),
                        hot[first : first + size, :],
                        part_of(own_ref, first, size, 2),
                        ends,
                    )
                    total = part if total is None else total + part
                sums.append(total)
            sum_ref[at, :] = jnp.where(halves[0], sums[0], sums[1])


def attend_own_call(own, bias_rows_in):
    return pl.pallas_call(
        attend_own_kernel,
        out_shape=(
            jax.ShapeDtypeStruct((2, 1024, 2 * LANES), BF16),
            jax.ShapeDtypeStruct((1024, LANES), F32),
        ),
        in_specs=[vmem(), vmem()],
        out_specs=(vmem(), vmem()),
        scratch_shapes=[pltpu.VMEM((1024, LANES), BF16)],
        cost_estimate=cost(2 * 1024 * 1024 * 512, 4 << 20),
        compiler_params=pltpu.CompilerParams(vmem_limit_bytes=ALL),
        name="attend_own",
    )(own, bias_rows_in)


def attend_prev_kernel(
    left_hbm, sum_hbm, prev_hbm, cache_k, cache_v, cache_b, out_hbm,
    left_ref, sum_ref, prev_ref, out_ref, keys, values, rows, hot, sems, in_sems, out_sems
):
    first = lax.axis_index("outer") == 0
    lanes = pl.ds(pl.multiple_of(lax.axis_index("side") * LANES, LANES), LANES)
    cached = (
        pltpu.make_async_copy(cache_k.at[:, lanes], keys, sems.at[0]),
        pltpu.make_async_copy(cache_v.at[:, lanes], values, sems.at[1]),
        pltpu.make_async_copy(cache_b, rows, sems.at[2]),
    )
    prev_copy = pltpu.make_async_copy(prev_hbm, prev_ref, in_sems.at[0])

    @pl.when(first)
    def _():
        started(*cached)

    @pl.when(jnp.logical_not(first))
    def _():
        prev_copy.start()

    left_copy, sum_copy = started(
        pltpu.make_async_copy(left_hbm, left_ref, in_sems.at[1]),
        pltpu.make_async_copy(sum_hbm, sum_ref, in_sems.at[2]),
    )

    @pl.when(first)
    def _():
        for copy in cached:
            copy.wait()

    @pl.when(jnp.logical_not(first))
    def _():
        prev_copy.wait()
        for s in range(8):
            at = slice(s * LANES, (s + 1) * LANES)
            rows[s : s + 1, :] = prev_ref[s, ROWS : ROWS + 1, 0:LANES].astype(F32).astype(jnp.int32)
            keys[at, :] = prev_ref[s, 0:ROWS, 0:LANES]
            values[at, :] = prev_ref[s, 0:ROWS, LANES : 2 * LANES]

    for s in range(8):
        at = slice(s * LANES, (s + 1) * LANES)
        hot[at, :] = hot_of(rows[s : s + 1, :].astype(F32))
    left_copy.wait()
    sum_copy.wait()
    lane = lax.broadcasted_iota(jnp.int32, (TILE, LANES), 1)
    sends = []
    for b in range(2):
        for t in range(2):
            start = b * 512 + t * TILE
            at = slice(start, start + TILE)
            sums = []
            for j in range(2):
                total = None
                for begin in (0, 512) if b == 0 else (512,):
                    span = slice(begin, begin + 512)
                    part = attended_sum(left_ref[j, at, :], keys[span, :], hot[span, :], values[span, :])
                    total = part if total is None else total + part
                sums.append(total)
            whole = sum_ref[at, :] + jnp.where(lane < NB, sums[0], sums[1])
            s = start // LANES
            out_ref[s : s + 2, :, :] = whole.astype(BF16).reshape(2, LANES, LANES)
            two = pl.ds(s, 2)
            sends += started(
                pltpu.make_async_copy(out_ref.at[two], out_hbm.at[two], out_sems.at[s // 2])
            )
    for copy in sends:
        copy.wait()


def attend_prev_call(left, partial, prev, prior_keys, prior_values, prior_buckets):
    return pl.pallas_call(
        attend_prev_kernel,
        out_shape=jax.ShapeDtypeStruct((8, ROWS, LANES), BF16),
        in_specs=[hbm()] * 6,
        out_specs=hbm(),
        scratch_shapes=[
            pltpu.VMEM(left.shape, BF16),
            pltpu.VMEM(partial.shape, F32),
            pltpu.VMEM(prev.shape, BF16),
            pltpu.VMEM((8, ROWS, LANES), BF16),
            pltpu.VMEM((1024, LANES), BF16),
            pltpu.VMEM((1024, LANES), BF16),
            pltpu.VMEM((8, LANES), jnp.int32),
            pltpu.VMEM((1024, LANES), BF16),
            pltpu.SemaphoreType.DMA((3,)),
            pltpu.SemaphoreType.DMA((3,)),
            pltpu.SemaphoreType.DMA((4,)),
        ],
        cost_estimate=cost(4 * 1024 * 1024 * 1024, 4 << 20),
        compiler_params=pltpu.CompilerParams(vmem_limit_bytes=61 << 20),
        name="attend_prev",
    )(left, partial, prev, prior_keys, prior_values, prior_buckets)


def mix_kernel(attended_ref, gate_ref, events_ref, w_ref, out_ref):
    parts = [attended_ref[(c % 2) * 4 + c // 2] for c in range(8)]
    whole = jnp.concatenate(parts, axis=1).astype(F32)
    gated = (standardised(whole) * gate_ref[...].astype(F32)).astype(BF16)
    mixed = events_ref[...].astype(F32) + jnp.dot(
        gated, w_ref[...], preferred_element_type=F32
    )
    out_ref[...] = mixed.astype(BF16)


def mix_call(attended, gate, events, w_output):
    return pl.pallas_call(
        mix_kernel,
        out_shape=jax.ShapeDtypeStruct(events.shape, BF16),
        in_specs=[vmem(), vmem(), vmem(), vmem()],
        out_specs=vmem(),
        cost_estimate=cost(2 << 27, 3 << 20),
        compiler_params=limited(8),
        name="mix",
    )(attended, gate, events, w_output)


def exchanged(parts):
    return lax.all_to_all(parts, RING, split_axis=0, concat_axis=0, tiled=True)


def per_device(
    events, buckets, counts, prior_keys, prior_values, prior_buckets, w_input, w_output, time_bias
):
    outer = lax.axis_size("outer")
    normed, sent = project_call(events, buckets.reshape(4, LANES), counts, w_input)
    earlier = lax.ppermute(normed, "outer", [(i, i + 1) for i in range(outer - 1)])
    own = exchanged(sent)
    gate = gate_call(normed, w_input)
    sent = project_prev_call(earlier, counts, w_input)

    def cached(own, sent, bias):
        left, partial = attend_own_call(own, bias)
        return left, partial, sent

    def received(own, sent, bias):
        prev = exchanged(sent)
        left, partial = attend_own_call(own, bias)
        return left, partial, prev

    left, partial, prev = lax.cond(
        lax.axis_index("outer") == 0, cached, received, own, sent, time_bias.T
    )
    attended = attend_prev_call(
        left, partial, prev, prior_keys, prior_values, prior_buckets.reshape(8, LANES)
    )
    attended = exchanged(attended)
    return mix_call(attended, gate, events, w_output)


def solution(mesh):
    rings = Mesh(
        mesh.devices.reshape(mesh.devices.shape[0] // 2, 2, mesh.devices.shape[1]),
        ("outer", "side", "narrow"),
    )
    placed = (
        P(("outer", "side", "narrow"), None),
        P(("outer", "side")),
        P(),
        P(None, "narrow"),
        P(None, "narrow"),
        P(),
        P(),
        P(),
        P(),
    )
    return jax.shard_map(
        per_device,
        mesh=rings,
        in_specs=placed,
        out_specs=P(("outer", "side", "narrow"), None),
        check_vma=False,
    )
```

```python
import jax
import jax.numpy as jnp
from jax import lax
from jax.experimental import pallas as pl
from jax.experimental.pallas import tpu as pltpu
from jax.sharding import Mesh, PartitionSpec as P


F32 = jnp.float32
BF16 = jnp.bfloat16
RING = ("side", "narrow")
ROWS = 128
LANES = 128
EXT = 136
NB = 64


def vmem():
    return pl.BlockSpec(memory_space=pltpu.VMEM)


def hbm():
    return pl.BlockSpec(memory_space=pltpu.HBM)


def limited(mib):
    return pltpu.CompilerParams(vmem_limit_bytes=mib << 20)


def cost(flops, moved):
    return pl.CostEstimate(flops=flops, bytes_accessed=moved, transcendentals=0)


def started(*copies):
    for copy in copies:
        copy.start()
    return copies


def silu_of_half(half):
    return half + half * jnp.tanh(half)


def standardised(values):
    mean = jnp.mean(values, axis=-1, keepdims=True)
    centred = values - mean
    var = jnp.mean(centred * centred, axis=-1, keepdims=True)
    return centred * lax.rsqrt(var + 1e-05)


STARTS = {"u": 0, "v": 1024, "q": 2048, "k": 3072}
ALL = 67_000_000
LAST = 53


def weight_copies(w_hbm, ws, sems, kinds):
    width = ws.shape[2]
    return [
        pltpu.make_async_copy(w_hbm.at[:, pl.ds(STARTS[kind], width)], ws.at[i], sems.at[i])
        for i, kind in enumerate(kinds)
    ]


def place_parts(part, kind, n, place, valid, out_ref):
    lanes = slice(place * LANES, (place + 1) * LANES)
    if kind == "q":
        part = part * 0.0625
    if kind == "v":
        part = jnp.where(valid, part, 0.0)
    part = part.astype(BF16)
    out_ref[n, 0:ROWS, lanes] = part[:, 0:LANES]
    out_ref[4 + n, 0:ROWS, lanes] = part[:, LANES:]


def valid_rows(lag, counts):
    block = 2 * (lax.axis_index("outer") - lag) + lax.axis_index("side")
    count = counts[jnp.maximum(block, 0)]
    at = lax.broadcasted_iota(jnp.int32, (ROWS, 2 * LANES), 0)
    return at + lax.axis_index("narrow") * ROWS < count


def tail_rows(x_ref, out_ref):
    tail = x_ref[ROWS:EXT, 0 : out_ref.shape[2]]
    for s in range(8):
        out_ref[s, ROWS:EXT, :] = tail


def project_kernel(
    events_hbm, buckets_hbm, counts_hbm, w_hbm, normed_hbm, out_hbm,
    events, buckets, counts, ws, normed, out, in_sems, w_sems, out_sems
):
    small = started(
        pltpu.make_async_copy(events_hbm, events, in_sems.at[0]),
        pltpu.make_async_copy(buckets_hbm, buckets, in_sems.at[1]),
        pltpu.make_async_copy(counts_hbm, counts, in_sems.at[2]),
    )
    weights = started(*weight_copies(w_hbm, ws, w_sems, "qkv"))
    for copy in small:
        copy.wait()
    x = standardised(events[...].astype(F32)).astype(BF16)
    normed[0:ROWS, :] = x
    own = buckets[pl.ds(lax.axis_index("narrow"), 1), :].astype(F32)
    width = normed.shape[1]
    row = jnp.concatenate([own] * (width // LANES), axis=1)
    normed[ROWS:EXT, :] = jnp.broadcast_to(row, (EXT - ROWS, width)).astype(BF16)
    sends = [pltpu.make_async_copy(normed, normed_hbm, out_sems.at[3])]
    sends[0].start()
    tail_rows(normed, out)
    valid = valid_rows(0, counts)
    for place, kind in enumerate("qkv"):
        weights[place].wait()
        for n in range(4):
            w = ws[place, :, n * 2 * LANES : (n + 1) * 2 * LANES]
            part = silu_of_half(0.5 * jnp.dot(x, w, preferred_element_type=F32))
            place_parts(part, kind, n, place, valid, out)
        lanes = pl.ds(place * LANES, LANES)
        sends += started(
            pltpu.make_async_copy(out.at[:, :, lanes], out_hbm.at[:, :, lanes], out_sems.at[place])
        )
    for copy in sends:
        copy.wait()


def project_call(events, buckets, counts, w_input):
    depth, width = w_input.shape
    return pl.pallas_call(
        project_kernel,
        out_shape=(
            jax.ShapeDtypeStruct((EXT, depth), BF16),
            jax.ShapeDtypeStruct((8, EXT, 3 * LANES), BF16),
        ),
        in_specs=[hbm()] * 4,
        out_specs=(hbm(), hbm()),
        scratch_shapes=[
            pltpu.VMEM((ROWS, depth), BF16),
            pltpu.VMEM((4, LANES), jnp.int32),
            pltpu.SMEM(counts.shape, jnp.int32),
            pltpu.VMEM((3, depth, 8 * LANES), BF16),
            pltpu.VMEM((EXT, depth), BF16),
            pltpu.VMEM((8, EXT, 3 * LANES), BF16),
            pltpu.SemaphoreType.DMA((3,)),
            pltpu.SemaphoreType.DMA((3,)),
            pltpu.SemaphoreType.DMA((4,)),
        ],
        cost_estimate=cost(2 * ROWS * depth * width, 2 * depth * width),
        compiler_params=pltpu.CompilerParams(vmem_limit_bytes=ALL),
        name="project_own",
    )(events, buckets, counts, w_input)


def project_prev_kernel(
    counts_hbm, x_hbm, w_hbm, out_hbm, counts, x, ws, out, in_sems, w_sems, out_sem
):
    small = started(
        pltpu.make_async_copy(x_hbm, x, in_sems.at[0]),
        pltpu.make_async_copy(counts_hbm, counts, in_sems.at[1]),
    )
    weights = started(*weight_copies(w_hbm, ws, w_sems, "kv"))
    for copy in small:
        copy.wait()
    valid = valid_rows(1, counts)
    tail_rows(x, out)
    for place, kind in enumerate("kv"):
        weights[place].wait()
        for n in range(4):
            w = ws[place, :, n * 2 * LANES : (n + 1) * 2 * LANES]
            dot = jnp.dot(x[0:ROWS, :], w, preferred_element_type=F32)
            place_parts(silu_of_half(0.5 * dot), kind, n, place, valid, out)
    send = pltpu.make_async_copy(out, out_hbm, out_sem)
    send.start()
    send.wait()


def project_prev_call(normed, counts, w_input):
    depth = w_input.shape[0]
    return pl.pallas_call(
        project_prev_kernel,
        out_shape=jax.ShapeDtypeStruct((8, EXT, 2 * LANES), BF16),
        in_specs=[hbm()] * 3,
        out_specs=hbm(),
        scratch_shapes=[
            pltpu.SMEM(counts.shape, jnp.int32),
            pltpu.VMEM((EXT, depth), BF16),
            pltpu.VMEM((2, depth, 8 * LANES), BF16),
            pltpu.VMEM((8, EXT, 2 * LANES), BF16),
            pltpu.SemaphoreType.DMA((2,)),
            pltpu.SemaphoreType.DMA((2,)),
            pltpu.SemaphoreType.DMA,
        ],
        cost_estimate=cost(4 * ROWS * depth * depth, 4 * depth * depth),
        compiler_params=pltpu.CompilerParams(vmem_limit_bytes=ALL),
        name="project_prev",
    )(counts, normed, w_input)


def gate_kernel(x_hbm, w_hbm, out_ref, x, ws, sems):
    copies = started(
        pltpu.make_async_copy(x_hbm, x, sems.at[0]),
        pltpu.make_async_copy(w_hbm.at[:, pl.ds(STARTS["u"], ws.shape[1])], ws, sems.at[1]),
    )
    for copy in copies:
        copy.wait()
    for n in range(4):
        lanes = slice(n * 2 * LANES, (n + 1) * 2 * LANES)
        half = 0.5 * jnp.dot(x[0:ROWS, :], ws[:, lanes], preferred_element_type=F32)
        out_ref[:, lanes] = silu_of_half(half).astype(BF16)


def gate_call(normed, w_input):
    depth = w_input.shape[0]
    return pl.pallas_call(
        gate_kernel,
        out_shape=jax.ShapeDtypeStruct((ROWS, depth), BF16),
        in_specs=[hbm(), hbm()],
        out_specs=vmem(),
        scratch_shapes=[
            pltpu.VMEM((EXT, depth), BF16),
            pltpu.VMEM((depth, depth), BF16),
            pltpu.SemaphoreType.DMA((2,)),
        ],
        cost_estimate=cost(2 * ROWS * depth * depth, 2 * depth * depth),
        compiler_params=pltpu.CompilerParams(vmem_limit_bytes=ALL),
        name="project_u",
    )(normed, w_input)


def hot_of(row):
    column = jnp.transpose(jnp.broadcast_to(row, (LANES, LANES)))
    lane = lax.broadcasted_iota(jnp.int32, (LANES, LANES), 1)
    wanted = jnp.where(lane >= NB, lane - NB, lane).astype(F32)
    return jnp.where(column == wanted, 1.0, 0.0).astype(BF16)


def bias_rows(bias_ref):
    at = lax.broadcasted_iota(jnp.int32, (NB, LANES), 1)
    gap = jnp.where(at <= NB, at, LANES - at)
    step = lax.broadcasted_iota(jnp.int32, (NB, LANES), 0)
    pick = jnp.where(gap == step, 1.0, 0.0).astype(F32)
    return 0.5 * lax.dot_general(
        bias_ref[...],
        pick,
        (((1,), (0,)), ((), ())),
        precision=lax.Precision.HIGHEST,
        preferred_element_type=F32,
    )


def pair_table(rows, head):
    at = lax.broadcasted_iota(jnp.int32, rows.shape, 0)
    row = jnp.sum(jnp.where(at == head, rows, 0.0), axis=0, keepdims=True)
    whole = jnp.broadcast_to(row, (NB, LANES))
    first = pltpu.roll(whole, 0, 1, stride=1, stride_axis=0)
    second = pltpu.roll(whole, NB, 1, stride=1, stride_axis=0)
    lane = lax.broadcasted_iota(jnp.int32, (NB, LANES), 1)
    coarse = first.astype(BF16)
    fine = (second - second.astype(BF16).astype(F32)).astype(BF16)
    table = jnp.where(lane < NB, coarse.astype(F32), fine.astype(F32))
    return jnp.concatenate([table, jnp.zeros_like(table)], axis=0).astype(BF16)


TILE = 256


def part_of(ref, start, size, place):
    s, n = start // LANES, size // LANES
    lanes = slice(place * LANES, (place + 1) * LANES)
    return ref[s : s + n, 0:ROWS, lanes].reshape(size, LANES)


def attended_sum(left, key, key_hot, value, ends=None):
    right = jnp.concatenate([key, key_hot], axis=1)
    half = lax.dot_general(left, right, (((1,), (1,)), ((), ())), preferred_element_type=F32)
    weight = silu_of_half(half)
    if ends is not None:
        r = lax.broadcasted_iota(jnp.int32, weight.shape, 0) + ends
        c = lax.broadcasted_iota(jnp.int32, weight.shape, 1)
        weight = jnp.where(c <= r, weight, 0.0)
    return jnp.dot(weight.astype(BF16), value, preferred_element_type=F32)


def attend_own_kernel(own_ref, bias_ref, left_ref, sum_ref, hot):
    for s in range(8):
        at = slice(s * LANES, (s + 1) * LANES)
        hot[at, :] = hot_of(own_ref[s, ROWS : ROWS + 1, 0:LANES].astype(F32))
    rows = bias_rows(bias_ref)
    head = lax.axis_index("narrow") * 4 + lax.axis_index("side") * 2
    tables = [pair_table(rows, head + j) for j in range(2)]
    lane = lax.broadcasted_iota(jnp.int32, (TILE, LANES), 1)
    halves = [lane < NB, lane >= NB]
    for b in range(2):
        for t in range(2):
            start = b * 512 + t * TILE
            at = slice(start, start + TILE)
            query = part_of(own_ref, start, TILE, 0).astype(F32)
            spans = [(0, 512, None)] if b == 1 else []
            if t == 1:
                spans.append((b * 512, TILE, None))
            spans.append((start, TILE, 0))
            sums = []
            for j in range(2):
                shifts = jnp.dot(hot[at, :], tables[j], preferred_element_type=F32).astype(BF16)
                mine = jnp.where(halves[j], query, 0.0).astype(BF16)
                left = jnp.concatenate([mine, shifts], axis=1)
                left_ref[j, at, :] = left
                total = None
                for first, size, ends in spans:
                    part = attended_sum(
                        left,
                        part_of(own_ref, first, size, 1),
                        hot[first : first + size, :],
                        part_of(own_ref, first, size, 2),
                        ends,
                    )
                    total = part if total is None else total + part
                sums.append(total)
            sum_ref[at, :] = jnp.where(halves[0], sums[0], sums[1])


def attend_own_call(own, bias_rows_in):
    return pl.pallas_call(
        attend_own_kernel,
        out_shape=(
            jax.ShapeDtypeStruct((2, 1024, 2 * LANES), BF16),
            jax.ShapeDtypeStruct((1024, LANES), F32),
        ),
        in_specs=[vmem(), vmem()],
        out_specs=(vmem(), vmem()),
        scratch_shapes=[pltpu.VMEM((1024, LANES), BF16)],
        cost_estimate=cost(2 * 1024 * 1024 * 512, 4 << 20),
        compiler_params=pltpu.CompilerParams(vmem_limit_bytes=ALL),
        name="attend_own",
    )(own, bias_rows_in)


def cache_kernel(cache_k, cache_v, cache_b, out_hbm, buckets, out, sems, out_sem):
    start = pl.multiple_of(lax.axis_index("side") * LANES, LANES)
    copies = [pltpu.make_async_copy(cache_b, buckets, sems.at[16])]
    for s in range(8):
        for place, cache in enumerate((cache_k, cache_v)):
            block = cache.at[pl.ds(s * ROWS, ROWS), pl.ds(start, LANES)]
            into = out.at[s, pl.ds(0, ROWS), pl.ds(place * LANES, LANES)]
            copies.append(pltpu.make_async_copy(block, into, sems.at[2 * s + place]))
    started(*copies)
    copies[0].wait()
    for s in range(8):
        row = buckets[s : s + 1, :].astype(F32)
        tail = jnp.broadcast_to(jnp.concatenate([row, row], axis=1), (EXT - ROWS, 2 * LANES))
        out[s, ROWS:EXT, :] = tail.astype(BF16)
    for copy in copies[1:]:
        copy.wait()
    send = pltpu.make_async_copy(out, out_hbm, out_sem)
    send.start()
    send.wait()


def cache_call(prior_keys, prior_values, prior_buckets):
    shape = (8, EXT, 2 * LANES)
    return pl.pallas_call(
        cache_kernel,
        out_shape=jax.ShapeDtypeStruct(shape, BF16),
        in_specs=[hbm()] * 3,
        out_specs=hbm(),
        scratch_shapes=[
            pltpu.VMEM((8, LANES), jnp.int32),
            pltpu.VMEM(shape, BF16),
            pltpu.SemaphoreType.DMA((17,)),
            pltpu.SemaphoreType.DMA,
        ],
        cost_estimate=cost(0, 2 << 20),
        compiler_params=pltpu.CompilerParams(vmem_limit_bytes=ALL),
        name="cached_blocks",
    )(prior_keys, prior_values, prior_buckets)


def attend_prev_kernel(
    left_hbm, sum_hbm, prev_hbm, out_hbm, left_ref, sum_ref, prev_ref, out_ref, hot, in_sems, out_sems
):
    prev_copy = pltpu.make_async_copy(prev_hbm, prev_ref, in_sems.at[8])
    prev_copy.start()
    tiles = []
    for i in range(4):
        rows = pl.ds(i * TILE, TILE)
        tiles.append(
            started(
                pltpu.make_async_copy(left_hbm.at[:, rows], left_ref.at[:, rows], in_sems.at[2 * i]),
                pltpu.make_async_copy(sum_hbm.at[rows], sum_ref.at[rows], in_sems.at[2 * i + 1]),
            )
        )
    prev_copy.wait()
    for s in range(8):
        at = slice(s * LANES, (s + 1) * LANES)
        hot[at, :] = hot_of(prev_ref[s, ROWS : ROWS + 1, 0:LANES].astype(F32))
    lane = lax.broadcasted_iota(jnp.int32, (TILE, LANES), 1)
    sends = []
    for i in range(4):
        at = slice(i * TILE, (i + 1) * TILE)
        for copy in tiles[i]:
            copy.wait()
        sums = []
        for j in range(2):
            total = None
            for begin in (0, 512) if i < 2 else (512,):
                part = attended_sum(
                    left_ref[j, at, :],
                    part_of(prev_ref, begin, 512, 0),
                    hot[begin : begin + 512, :],
                    part_of(prev_ref, begin, 512, 1),
                )
                total = part if total is None else total + part
            sums.append(total)
        whole = sum_ref[at, :] + jnp.where(lane < NB, sums[0], sums[1])
        out_ref[2 * i : 2 * i + 2, :, :] = whole.astype(BF16).reshape(2, LANES, LANES)
        two = pl.ds(2 * i, 2)
        sends += started(pltpu.make_async_copy(out_ref.at[two], out_hbm.at[two], out_sems.at[i]))
    for copy in sends:
        copy.wait()


def attend_prev_call(left, partial, prev):
    return pl.pallas_call(
        attend_prev_kernel,
        out_shape=jax.ShapeDtypeStruct((8, ROWS, LANES), BF16),
        in_specs=[hbm()] * 3,
        out_specs=hbm(),
        scratch_shapes=[
            pltpu.VMEM(left.shape, BF16),
            pltpu.VMEM(partial.shape, F32),
            pltpu.VMEM(prev.shape, BF16),
            pltpu.VMEM((8, ROWS, LANES), BF16),
            pltpu.VMEM((1024, LANES), BF16),
            pltpu.SemaphoreType.DMA((9,)),
            pltpu.SemaphoreType.DMA((4,)),
        ],
        cost_estimate=cost(4 * 1024 * 1024 * 1024, 4 << 20),
        compiler_params=limited(LAST),
        name="attend_prev",
    )(left, partial, prev)


def mix_kernel(attended_ref, gate_ref, events_ref, w_ref, out_ref):
    parts = [attended_ref[(c % 2) * 4 + c // 2] for c in range(8)]
    whole = jnp.concatenate(parts, axis=1).astype(F32)
    gated = (standardised(whole) * gate_ref[...].astype(F32)).astype(BF16)
    mixed = events_ref[...].astype(F32) + jnp.dot(
        gated, w_ref[...], preferred_element_type=F32
    )
    out_ref[...] = mixed.astype(BF16)


def mix_call(attended, gate, events, w_output):
    return pl.pallas_call(
        mix_kernel,
        out_shape=jax.ShapeDtypeStruct(events.shape, BF16),
        in_specs=[vmem(), vmem(), vmem(), vmem()],
        out_specs=vmem(),
        cost_estimate=cost(2 << 27, 3 << 20),
        compiler_params=limited(8),
        name="mix",
    )(attended, gate, events, w_output)


def exchanged(parts):
    return lax.all_to_all(parts, RING, split_axis=0, concat_axis=0, tiled=True)


def per_device(
    events, buckets, counts, prior_keys, prior_values, prior_buckets, w_input, w_output, time_bias
):
    outer = lax.axis_size("outer")
    normed, sent = project_call(events, buckets.reshape(4, LANES), counts, w_input)
    earlier = lax.ppermute(normed, "outer", [(i, i + 1) for i in range(outer - 1)])
    own = exchanged(sent)
    gate = gate_call(normed, w_input)
    sent = project_prev_call(earlier, counts, w_input)

    def cached(own, sent, bias, *prior):
        left, partial = attend_own_call(own, bias)
        return left, partial, cache_call(*prior)

    def received(own, sent, bias, *prior):
        prev = exchanged(sent)
        left, partial = attend_own_call(own, bias)
        return left, partial, prev

    prior = (prior_keys, prior_values, prior_buckets.reshape(8, LANES))
    left, partial, prev = lax.cond(
        lax.axis_index("outer") == 0, cached, received, own, sent, time_bias.T, *prior
    )
    attended = attend_prev_call(left, partial, prev)
    attended = exchanged(attended)
    return mix_call(attended, gate, events, w_output)


def solution(mesh):
    rings = Mesh(
        mesh.devices.reshape(mesh.devices.shape[0] // 2, 2, mesh.devices.shape[1]),
        ("outer", "side", "narrow"),
    )
    placed = (
        P(("outer", "side", "narrow"), None),
        P(("outer", "side")),
        P(),
        P(None, "narrow"),
        P(None, "narrow"),
        P(),
        P(),
        P(),
        P(),
    )
    return jax.shard_map(
        per_device,
        mesh=rings,
        in_specs=placed,
        out_specs=P(("outer", "side", "narrow"), None),
        check_vma=False,
    )
```
